32 devices in a mesh: tile: 16 (over z, x, core), group: 2 (over y).
Axes of the slice: x: 2, y: 2, z: 4, core: 2. Of those that a mesh axis runs over, the one named last changes fastest.
Arguments:
- object_field: float32 [2, 320, 2048], P(None, 'group', 'tile'), may hold values from -6 to 6
- probe_field: float32 [2, 256, 256], replicated, may hold values from -6 to 6
- amplitudes: float32 [32, 256, 256], P(('tile', 'group')), may hold values from 0 to 4
- row_start: int32 [32], P(('tile', 'group')), may hold values from 0 to 64
- column_start: int32 [32], P(('tile', 'group')), may hold values from 0 to 128
- live_slots: int32 [32], P(('tile', 'group')), may hold values 0 or 1
Outputs:
- new_object: float32 [2, 320, 2048], P(None, 'group', 'tile')
- new_probe: float32 [2, 256, 256], replicated
The draws below stay inside these ranges and needn't reach their ends.
All inputs are finite; a program needn't handle non-finite values. No bound on the sum of `live_slots` on one device may be relied on, other than what follows from the above.
Results may differ from the reference program's by a relative error of at most 0.0001.
Values sent between devices are 32-bit elements; how exact they have to be, the bound alone decides.
A program may use at most 64 MiB of HBM per device.

```python
import math
import jax
import jax.numpy as jnp
from jax import lax

WIN = 256
HALO = 128
ITERS = 1
OBJ_ROWS = 320
COLS_DEV = 128
POS_DEV = 1
OBJ_COLS = 2048
POSITIONS = 32
N_TILE = 16
N_GROUP = 2


def with_ends(drawn, own_key, smallest, top_value):
    longest = drawn.shape.index(max(drawn.shape))
    spots = []
    for shift in (0, 1):
        where = [jax.random.randint(jax.random.fold_in(own_key, axis), (), 0, length) for axis, length in enumerate(drawn.shape)]
        where[longest] = (where[longest] + shift) % drawn.shape[longest]
        spots.append(tuple(where))
    return drawn.at[spots[0]].set(smallest).at[spots[1]].set(top_value)


def shard_levels(stream_key, extent, split, least, top_value):
    def one(position, shards_of):
        steps = jax.random.uniform(jax.random.fold_in(jax.random.fold_in(stream_key, 6), position), (shards_of,), jnp.float32, least / len(split), top_value / len(split))
        return jnp.repeat(jnp.exp(steps), extent[position] // shards_of).reshape((-1,) + (1,) * (len(extent) - position - 1))

    gain = one(*split[0])
    for cut in split[1:]:
        gain = gain * one(*cut)
    return gain


def normal_values(key, dims, spread, most, pieces=(), held_as=jnp.bfloat16):
    drawn = jax.random.normal(key, dims, jnp.float32) * spread
    if len(pieces) > 0:
        drawn = shard_levels(key, dims, pieces, -0.22, 0.18) * drawn
    return jnp.clip(drawn, min=-most, max=most).astype(held_as)


def setup_inputs(seed: int = 0) -> dict:
    arg_keys = jax.random.split(jax.random.key(seed), 7)
    object_field = normal_values(arg_keys[0], (2, OBJ_ROWS, OBJ_COLS), 1.0, 6.0, ((1, 2), (2, 16)), jnp.float32)
    probe_field = normal_values(arg_keys[1], (2, WIN, WIN), 1.0, 6.0, (), jnp.float32)
    amplitudes = jnp.clip(4.0 * jax.random.uniform(arg_keys[2], (POSITIONS, WIN, WIN), jnp.float32) ** shard_levels(arg_keys[2], (POSITIONS, WIN, WIN), ((0, 32),), -0.2, 0.2), 0.0, 4.0)
    row_start = with_ends(jax.random.randint(arg_keys[3], (POSITIONS,), 0, OBJ_ROWS - WIN + 1), jax.random.fold_in(arg_keys[3], 1), 0, OBJ_ROWS - WIN).astype(jnp.int32)
    column_start = with_ends(jax.random.randint(arg_keys[4], (POSITIONS,), 0, COLS_DEV + 2 * HALO - WIN + 1), jax.random.fold_in(arg_keys[4], 1), 0, COLS_DEV + 2 * HALO - WIN).astype(jnp.int32)
    live_slots = with_ends((jax.random.randint(arg_keys[5], (POSITIONS,), 0, 4) < 3).astype(jnp.int32), jax.random.fold_in(arg_keys[5], 1), 0, 1)
    return dict(object_field=object_field, probe_field=probe_field, amplitudes=amplitudes, row_start=row_start, column_start=column_start, live_slots=live_slots)


def dft_tables(length):
    counter = jnp.arange(length, dtype=jnp.int32)
    product = counter[:, None] * counter[None, :] % length
    angles = 2.0 * math.pi / length * product.astype(jnp.float32)
    factor = 1.0 / math.sqrt(length)
    return (jnp.cos(angles) * factor, jnp.sin(angles) * factor)

def apply_left(matrix, values):
    return jnp.einsum('jk,pkl->pjl', matrix, values, precision=lax.Precision.HIGHEST)

def apply_right(values, matrix):
    return jnp.einsum('pjk,kl->pjl', values, matrix, precision=lax.Precision.HIGHEST)

def transform(real_part, imag_part, cos_table, sin_table, sign):
    left_real = apply_left(cos_table, real_part) - sign * apply_left(sin_table, imag_part)
    left_imag = apply_left(cos_table, imag_part) + sign * apply_left(sin_table, real_part)
    right_real = apply_right(left_real, cos_table) - sign * apply_right(left_imag, sin_table)
    right_imag = apply_right(left_imag, cos_table) + sign * apply_right(left_real, sin_table)
    return (right_real, right_imag)

def window_terms(windows, probe_field, amplitudes, live_slots, cos_table, sin_table):
    sample_real = windows[:, 0]
    sample_imag = windows[:, 1]
    probe_real = probe_field[0]
    probe_imag = probe_field[1]
    exit_real = probe_real * sample_real - probe_imag * sample_imag
    exit_imag = probe_real * sample_imag + probe_imag * sample_real
    far_real, far_imag = transform(exit_real, exit_imag, cos_table, sin_table, -1.0)
    modulus = jnp.maximum(jnp.sqrt(far_real * far_real + far_imag * far_imag), 0.25)
    factor = 1.0 - amplitudes / modulus
    miss_real, miss_imag = transform(far_real * factor, far_imag * factor, cos_table, sin_table, 1.0)
    weight = live_slots.astype(jnp.float32)[:, None, None]
    miss_real = miss_real * weight
    miss_imag = miss_imag * weight
    grad_real = probe_real * miss_real + probe_imag * miss_imag
    grad_imag = probe_real * miss_imag - probe_imag * miss_real
    probe_light = weight * (probe_real * probe_real + probe_imag * probe_imag)
    terms = jnp.stack([grad_real, grad_imag, probe_light], axis=1)
    probe_grad = jnp.stack([lax.optimization_barrier(jnp.sum(sample_real * miss_real + sample_imag * miss_imag, axis=0)), lax.optimization_barrier(jnp.sum(sample_real * miss_imag - sample_imag * miss_real, axis=0))], axis=0)
    window_light = lax.optimization_barrier(jnp.sum(weight * (sample_real * sample_real + sample_imag * sample_imag), axis=0))
    return (terms, probe_grad, window_light)

def add_windows(accum, terms, top_rows, left_edges):
    zero_index = jnp.zeros((), jnp.int32)

    def place(slot, current):
        corner = (zero_index, top_rows[slot], left_edges[slot])
        piece = lax.dynamic_slice(current, corner, (3, WIN, WIN))
        return lax.dynamic_update_slice(current, piece + terms[slot], corner)
    return lax.fori_loop(0, terms.shape[0], place, accum)

def cut_windows(padded, top_rows, left_edges):
    zero_index = jnp.zeros((), jnp.int32)

    def single(top_row, left_edge):
        return lax.dynamic_slice(padded, (zero_index, top_row, left_edge), (2, WIN, WIN))
    return jax.vmap(single)(top_rows, left_edges)

def apply_updates(object_field, probe_field, share, probe_grad, window_light):
    light_max = jnp.max(probe_field[0] * probe_field[0] + probe_field[1] * probe_field[1]) + 1e-06
    new_object = object_field - share[0:2] / (share[2:3] + 0.25 * light_max)
    new_probe = probe_field - probe_grad / (window_light + 0.25 * jnp.mean(window_light) + 1e-05)[None]
    return (new_object, new_probe)

def reference(object_field, probe_field, amplitudes, row_start, column_start, live_slots):
    cos_table, sin_table = dft_tables(WIN)
    blocks = N_TILE * N_GROUP
    tile_first = jnp.arange(blocks, dtype=jnp.int32) // N_GROUP * COLS_DEV
    block_cols = (column_start.reshape(blocks, POS_DEV).astype(jnp.int32) + tile_first[:, None]).astype(jnp.int32)
    block_rows = row_start.reshape(blocks, POS_DEV).astype(jnp.int32)
    block_amps = amplitudes.reshape(blocks, POS_DEV, WIN, WIN)
    block_live = live_slots.reshape(blocks, POS_DEV)
    for iteration in range(ITERS):
        padded = jnp.pad(object_field, ((0, 0), (0, 0), (HALO, HALO)))

        def visit(carry, block):
            grad_acc, probe_acc, light_acc = carry
            top_rows, left_edges, amps_here, live_here = block
            windows = cut_windows(padded, top_rows, left_edges)
            terms, probe_grad, window_light = window_terms(windows, probe_field, amps_here, live_here, cos_table, sin_table)
            grad_acc = add_windows(grad_acc, terms, top_rows, left_edges)
            return ((grad_acc, probe_acc + probe_grad, light_acc + window_light), None)
        start = (jnp.zeros((3, OBJ_ROWS, OBJ_COLS + 2 * HALO), jnp.float32), jnp.zeros((2, WIN, WIN), jnp.float32), jnp.zeros((WIN, WIN), jnp.float32))
        (grad_acc, probe_grad, window_light), unused = lax.scan(visit, start, (block_rows, block_cols, block_amps, block_live))
        share = grad_acc[:, :, HALO:HALO + OBJ_COLS]
        object_field, probe_field = apply_updates(object_field, probe_field, share, probe_grad, window_light)
    return (object_field, probe_field)
```

```python
import functools
import math

import jax
import jax.numpy as jnp
import numpy as np
from jax import lax
from jax.experimental import pallas as pl
from jax.experimental.pallas import tpu as pltpu
from jax.sharding import PartitionSpec as P

MESH = pl.DeviceIdType.MESH
F32 = jnp.float32
BF16 = jnp.bfloat16


def dft_tables(length):
    k = np.arange(length)
    angles = 2.0 * math.pi / length * (np.outer(k, k) % length)
    cos, sin = np.cos(angles) / math.sqrt(length), np.sin(angles) / math.sqrt(length)
    full = np.block([[cos, sin], [-sin, cos]]).astype(np.float32)
    head = full.astype(BF16)
    tail = (full - head.astype(np.float32)).astype(BF16)
    return head, tail


def split(x):
    head = x.astype(BF16)
    return head, (x - head.astype(F32)).astype(BF16)


def mm(a, b):
    return jnp.dot(a, b, preferred_element_type=F32)


def table_left(head, tail, x):
    xh, xl = split(x)
    return mm(head, xh) + (mm(head, xl) + mm(tail, xh))


def table_right(x, head, tail):
    xh, xl = split(x)
    return mm(xh, head) + (mm(xl, head) + mm(xh, tail))


def remote(src, dst, send, recv, tile, group):
    return pltpu.make_async_remote_copy(
        src_ref=src, dst_ref=dst, send_sem=send, recv_sem=recv,
        device_id={"tile": tile, "group": group}, device_id_type=MESH,
    )


class AllReduce:
    def __init__(self, plan, part, pair, mine, came, full, sems):
        self.p, self.part, self.pair, self.mine = plan, part, pair, mine
        self.came, self.full, self.sems = came, full, sems

    def pair_copy(self):
        p = self.p
        return remote(self.part.at[1 - p.h, p.s], self.pair, self.sems[0].at[0],
                      self.sems[1].at[0], p.partner, p.g)

    def spread_copy(self, d):
        p = self.p
        to = lax.rem(p.k + d, p.H)
        return remote(self.mine.at[to], self.came.at[d - 1], self.sems[2].at[d - 1],
                      self.sems[3].at[d - 1], 2 * to + p.h, p.g)

    def collect_copy(self, dg, dk, arriving):
        p = self.p
        n = dg * p.H + dk
        sign = -1 if arriving else 1
        k = lax.rem(p.k + sign * dk + p.H, p.H)
        s = lax.rem(p.s + sign * dg + p.gs, p.gs)
        slot = self.full.at[p.h, s, k] if arriving else self.full.at[p.h, p.s, p.k]
        return remote(slot, slot, self.sems[4].at[n], self.sems[5].at[n],
                      2 * k + p.h, p.g - p.s + s)

    def relay_copy(self, dg, dk, arriving):
        p = self.p
        n = dg * p.H + dk
        k = lax.rem(p.k - dk + p.H, p.H)
        s = lax.rem(p.s - dg + p.gs, p.gs)
        h = 1 - p.h if arriving else p.h
        slot = self.full.at[h, s, k]
        return remote(slot, slot, self.sems[6].at[n], self.sems[7].at[n], p.partner, p.g)

    def others(self):
        p = self.p
        return [(dg, dk) for dk in range(p.H) for dg in range(p.gs) if dg or dk]

    def put(self, channel, value):
        p = self.p
        self.part[:, :, :, channel] = value.reshape(2, p.gs, p.H, p.rows, value.shape[-1])

    def start_pair(self):
        self.pair_copy().start()

    def start_spread(self):
        p = self.p
        self.pair_copy().wait()
        self.mine[...] = self.part[p.h, p.s] + self.pair[...]
        for d in range(1, p.H):
            self.spread_copy(d).start()

    def start_collect(self):
        p = self.p
        total = self.mine[p.k]
        for d in range(1, p.H):
            self.spread_copy(d).wait()
            total = total + self.came[d - 1]
        self.full[p.h, p.s, p.k] = total
        for dg, dk in self.others():
            self.collect_copy(dg, dk, False).start()
        self.relay_copy(0, 0, False).start()

    def relay(self):
        for dg, dk in self.others():
            self.collect_copy(dg, dk, True).wait_recv()
            self.relay_copy(dg, dk, False).start()

    def finish(self):
        self.relay_copy(0, 0, True).wait_recv()
        self.relay_copy(0, 0, False).wait_send()
        for dg, dk in self.others():
            self.relay_copy(dg, dk, True).wait_recv()
            self.relay_copy(dg, dk, False).wait_send()
            self.collect_copy(dg, dk, False).wait_send()

    def get(self, channel):
        whole = self.full[:, :, :, channel]
        return whole.reshape(-1, whole.shape[-1])


class Plan:
    pass


def kernel(T, G, gs, obj, probe, amp, scal_in, a_head, a_tail, b_head, b_tail,
           new_obj, new_probe, pad, amps, scal, win, terms, light_terms, acc, acc_light,
           edge, edge_light, grad_sum, *rest):
    t, g = lax.axis_index("tile"), lax.axis_index("group")
    R, W = obj.shape[1], probe.shape[1]
    B = obj.shape[2]
    rows = pad.shape[2]
    p = Plan()
    p.g, p.H, p.gs = g, T // 2, gs
    p.k, p.h = lax.div(t, 2), lax.rem(t, 2)
    p.partner = t + 1 - 2 * p.h
    p.s = lax.rem(g, gs)
    p.rows = W // 2 // (p.H * gs)
    light_red = AllReduce(p, *rest[0:5], rest[5:13])
    grad_red = AllReduce(p, *rest[13:18], rest[18:26])
    (own_s, own_r, side_s, side_r, amp_s, amp_r, scal_s, scal_r,
     edge_s, edge_r) = rest[26:36]

    barrier = pltpu.get_barrier_semaphore()
    count = 0
    for dt in range(T):
        for dg in range(G):
            same_block = G == gs
            if (dt or dg) and (same_block or dt == 0 or dg == 0):
                pl.semaphore_signal(
                    barrier, inc=1,
                    device_id={"tile": lax.rem(t + dt, T), "group": lax.rem(g + dg, G)},
                    device_id_type=MESH)
                count += 1
    pl.semaphore_wait(barrier, count)

    def span(group):
        return pl.ds(pl.multiple_of(group * R, 8), R)

    def to_peer(j, arriving):
        peer = lax.rem(g + (G - j if arriving else j), G)
        slot = pad.at[1, :, span(peer if arriving else g)]
        return remote(slot if arriving else obj, slot, own_s.at[j - 1], own_r.at[j - 1], t, peer)

    def to_side(j, right, arriving):
        who = lax.rem(g + G - j, G)
        block = (0 if right else 2)
        dst = pad.at[block, :, span(who)]
        src = obj if j == 0 else pad.at[1, :, span(who)]
        n = 2 * j + int(right)
        return remote(dst if arriving else src, dst, side_s.at[n], side_r.at[n],
                      (t + 1 if right else t - 1) if not arriving else (t - 1 if right else t + 1), g)

    def amp_copy(j, arriving):
        peer = lax.rem(g + (G - j if arriving else j), G)
        slot = amps.at[peer if arriving else g]
        return remote(slot if arriving else amp.at[0], slot, amp_s.at[j - 1], amp_r.at[j - 1], t, peer)

    def scal_copy(j, arriving):
        peer = lax.rem(g + (G - j if arriving else j), G)
        slot = scal.at[peer if arriving else g]
        return remote(slot if arriving else scal_in, slot, scal_s.at[j - 1], scal_r.at[j - 1], t, peer)

    def edge_copy(src, dst, right, base, arriving):
        n = base + int(right)
        side = dst.at[0 if right else 1]
        if arriving:
            return remote(side, side, edge_s.at[n], edge_r.at[n], t - 1 if right else t + 1, g)
        return remote(src.at[2 if right else 0], side, edge_s.at[n], edge_r.at[n],
                      t + 1 if right else t - 1, g)

    not_first, not_last = t > 0, t < T - 1

    for j in range(1, G):
        to_peer(j, False).start()
    pl.when(not_first)(lambda: to_side(0, False, False).start())
    pl.when(not_last)(lambda: to_side(0, True, False).start())
    for j in range(1, G):
        scal_copy(j, False).start()
    for j in range(1, G):
        amp_copy(j, False).start()

    pad[1, :, span(g)] = obj[...]
    scal[g] = scal_in[...]
    amps[g] = amp[0]

    @pl.when(t == 0)
    def _():
        pad[0] = jnp.zeros(pad.shape[1:], F32)
        edge[0] = jnp.zeros(edge.shape[1:], F32)
        edge_light[0] = jnp.zeros(edge_light.shape[1:], F32)

    @pl.when(t == T - 1)
    def _():
        pad[2] = jnp.zeros(pad.shape[1:], F32)
        edge[1] = jnp.zeros(edge.shape[1:], F32)
        edge_light[1] = jnp.zeros(edge_light.shape[1:], F32)

    spare = rows - W
    blocks = W // B
    terms[:, :, 0:spare] = jnp.zeros((2, blocks, spare, B), F32)
    terms[:, :, spare + W:] = jnp.zeros((2, blocks, spare, B), F32)
    light_terms[:, 0:spare] = jnp.zeros((blocks, spare, B), F32)
    light_terms[:, spare + W:] = jnp.zeros((blocks, spare, B), F32)

    def hold(ref, value):
        for b in range(blocks):
            ref[b, spare:spare + W] = value[:, b * B:(b + 1) * B]

    probe_light = probe[0] * probe[0] + probe[1] * probe[1]
    hold(light_terms, probe_light)
    light_max = jnp.max(probe_light) + 1e-06

    for j in range(1, G):
        to_peer(j, True).wait_recv()
        pl.when(not_first)(lambda: to_side(j, False, False).start())
        pl.when(not_last)(lambda: to_side(j, True, False).start())
    for j in range(1, G):
        scal_copy(j, True).wait_recv()
    for j in range(G):
        pl.when(not_last)(lambda: to_side(j, False, True).wait_recv())
        pl.when(not_first)(lambda: to_side(j, True, True).wait_recv())

    def numbers(k):
        return scal[k, 0, 0], scal[k, 1, 0], scal[k, 2, 0].astype(F32)

    def placed(ref, row, column):
        first = g * R + spare - row
        pieces = [ref[b, pl.ds(first, R), :] for b in range(blocks)]
        wide = jnp.concatenate(pieces + [jnp.zeros((R, 3 * B - W), F32)], axis=1)
        return pltpu.roll(wide, column, 1)

    acc[...] = jnp.zeros(acc.shape, F32)
    acc_light[...] = jnp.zeros(acc_light.shape, F32)
    grad_sum[...] = jnp.zeros(grad_sum.shape, F32)

    def look(j, light):
        k = lax.rem(g + j, G)
        row, column, weight = numbers(k)
        for ch in range(2):
            wide = jnp.concatenate([pad[b, ch, pl.ds(row, W), :] for b in range(3)], axis=1)
            win[k, ch] = pltpu.roll(wide, lax.rem(3 * B - column, 3 * B), 1)[:, 0:W]
        spread = weight * placed(light_terms, row, column)
        for b in range(3):
            acc_light[b] += spread[:, b * B:(b + 1) * B]
        return light + weight * (win[k, 0] * win[k, 0] + win[k, 1] * win[k, 1])

    light = lax.fori_loop(0, G, look, jnp.zeros((W, W), F32))
    light_red.put(0, light)
    light_red.start_pair()
    pl.when(not_first)(lambda: edge_copy(acc_light, edge_light, False, 0, False).start())
    pl.when(not_last)(lambda: edge_copy(acc_light, edge_light, True, 0, False).start())

    def position(k):
        row, column, weight = numbers(k)
        wr, wi = win[k, 0], win[k, 1]
        pr, pi = probe[0], probe[1]
        x = jnp.concatenate([pr * wr - pi * wi, pr * wi + pi * wr], axis=0)
        y = table_left(a_head[...], a_tail[...], x)
        z = table_right(jnp.concatenate([y[:W], y[W:]], axis=1), b_head[...], b_tail[...])
        zr, zi = z[:, :W], z[:, W:]
        factor = 1.0 - amps[k] * lax.rsqrt(jnp.maximum(zr * zr + zi * zi, 0.0625))
        x = jnp.concatenate([zr * factor, zi * factor], axis=0)
        y = table_left(b_head[...], b_tail[...], x)
        z = table_right(jnp.concatenate([y[:W], y[W:]], axis=1), a_head[...], a_tail[...])
        mr, mi = z[:, :W] * weight, z[:, W:] * weight
        hold(terms.at[0], pr * mr + pi * mi)
        hold(terms.at[1], pr * mi - pi * mr)
        grad_sum[0] += wr * mr + wi * mi
        grad_sum[1] += wr * mi - wi * mr
        for ch in range(2):
            spread = placed(terms.at[ch], row, column)
            for b in range(3):
                acc[b, ch] += spread[:, b * B:(b + 1) * B]

    position(g)
    light_red.start_spread()
    for j in range(1, G):
        amp_copy(j, True).wait_recv()
    pl.loop(1, G)(lambda j: position(lax.rem(g + j, G)))

    for ch in range(2):
        grad_red.put(ch, grad_sum[ch])
    grad_red.start_pair()
    light_red.start_collect()
    grad_red.start_spread()
    pl.when(not_first)(lambda: edge_copy(acc, edge, False, 2, False).start())
    pl.when(not_last)(lambda: edge_copy(acc, edge, True, 2, False).start())
    light_red.relay()
    grad_red.start_collect()

    for src, dst, base in ((acc_light, edge_light, 0), (acc, edge, 2)):
        pl.when(not_last)(lambda: edge_copy(src, dst, False, base, True).wait_recv())
        pl.when(not_first)(lambda: edge_copy(src, dst, True, base, True).wait_recv())
    below = 1.0 / (acc_light[1] + edge_light[0] + edge_light[1] + 0.25 * light_max)
    for ch in range(2):
        new_obj[ch] = obj[ch] - (acc[1, ch] + edge[0, ch] + edge[1, ch]) * below
    light_red.finish()
    light = light_red.get(0)
    below = 1.0 / (light + 0.25 * jnp.mean(light) + 1e-05)
    grad_red.relay()
    grad_red.finish()
    for ch in range(2):
        new_probe[ch] = probe[ch] - grad_red.get(ch) * below

    for j in range(1, G):
        to_peer(j, False).wait_send()
        amp_copy(j, False).wait_send()
        scal_copy(j, False).wait_send()
    for j in range(G):
        pl.when(not_first)(lambda: to_side(j, False, False).wait_send())
        pl.when(not_last)(lambda: to_side(j, True, False).wait_send())
    for src, dst, base in ((acc_light, edge_light, 0), (acc, edge, 2)):
        pl.when(not_first)(lambda: edge_copy(src, dst, False, base, False).wait_send())
        pl.when(not_last)(lambda: edge_copy(src, dst, True, base, False).wait_send())


def local(T, G, object_field, probe_field, amplitudes, row_start, column_start, live_slots):
    R, B = object_field.shape[1:]
    W = probe_field.shape[1]
    rows = R * G
    H = T // 2
    gs = max(n for n in range(1, G + 1) if G % n == 0 and n * H * 8 <= W // 2)
    chunk = W // 2 // (H * gs)
    head, tail = dft_tables(W)
    scal = jnp.concatenate([row_start, column_start, live_slots, live_slots]).astype(jnp.int32)
    scal = jnp.broadcast_to(jnp.concatenate([scal, scal])[:, None], (8, 128))
    spare = rows - W
    dma = lambda n: pltpu.SemaphoreType.DMA((max(n, 1),))

    def reduce_scratch(channels):
        return [
            pltpu.VMEM((2, gs, H, channels, chunk, W), F32),
            pltpu.VMEM((H, channels, chunk, W), F32),
            pltpu.VMEM((H, channels, chunk, W), F32),
            pltpu.VMEM((H - 1, channels, chunk, W), F32),
            pltpu.VMEM((2, gs, H, channels, chunk, W), F32),
            dma(1), dma(1), dma(H - 1), dma(H - 1), dma(gs * H), dma(gs * H), dma(gs * H), dma(gs * H),
        ]

    vmem = pl.BlockSpec(memory_space=pltpu.VMEM)
    return pl.pallas_call(
        functools.partial(kernel, T, G, gs),
        out_shape=(jax.ShapeDtypeStruct(object_field.shape, F32),
                   jax.ShapeDtypeStruct(probe_field.shape, F32)),
        in_specs=[vmem] * 8,
        out_specs=(vmem, vmem),
        scratch_shapes=[
            pltpu.VMEM((3, 2, rows, B), F32),
            pltpu.VMEM((G, W, W), F32),
            pltpu.VMEM((G, 8, 128), jnp.int32),
            pltpu.VMEM((G, 2, W, W), F32),
            pltpu.VMEM((2, W // B, W + 2 * spare, B), F32),
            pltpu.VMEM((W // B, W + 2 * spare, B), F32),
            pltpu.VMEM((3, 2, R, B), F32),
            pltpu.VMEM((3, R, B), F32),
            pltpu.VMEM((2, 2, R, B), F32),
            pltpu.VMEM((2, R, B), F32),
            pltpu.VMEM((2, W, W), F32),
            *reduce_scratch(1),
            *reduce_scratch(2),
            dma(G - 1), dma(G - 1), dma(2 * G), dma(2 * G), dma(G - 1), dma(G - 1),
            dma(G - 1), dma(G - 1), dma(4), dma(4),
        ],
        compiler_params=pltpu.CompilerParams(
            collective_id=0, has_side_effects=True, vmem_limit_bytes=60 * 1024 * 1024),
    )(object_field, probe_field, amplitudes, scal, head, tail, head.T, tail.T)


def solution(mesh):
    return jax.shard_map(
        functools.partial(local, mesh.shape["tile"], mesh.shape["group"]),
        mesh=mesh,
        in_specs=(
            P(None, "group", "tile"),
            P(),
            P(("tile", "group"), None, None),
            P(("tile", "group")),
            P(("tile", "group")),
            P(("tile", "group")),
        ),
        out_specs=(P(None, "group", "tile"), P()),
        check_vma=False,
    )
```

```python
import functools
import math

import jax
import jax.numpy as jnp
import numpy as np
from jax import lax
from jax.experimental import pallas as pl
from jax.experimental.pallas import tpu as pltpu
from jax.sharding import PartitionSpec as P

MESH = pl.DeviceIdType.MESH
F32 = jnp.float32
BF16 = jnp.bfloat16


def dft_tables(length):
    k = np.arange(length)
    angles = 2.0 * math.pi / length * (np.outer(k, k) % length)
    cos, sin = np.cos(angles) / math.sqrt(length), np.sin(angles) / math.sqrt(length)
    full = np.block([[cos, sin], [-sin, cos]]).astype(np.float32)
    head = full.astype(BF16)
    tail = (full - head.astype(np.float32)).astype(BF16)
    return head, tail


def split(x):
    head = x.astype(BF16)
    return head, (x - head.astype(F32)).astype(BF16)


def mm(a, b):
    return jnp.dot(a, b, preferred_element_type=F32)


def table_left(head, tail, x):
    xh, xl = split(x)
    return mm(head, xh) + (mm(head, xl) + mm(tail, xh))


def table_right(x, head, tail):
    xh, xl = split(x)
    return mm(xh, head) + (mm(xl, head) + mm(xh, tail))


def remote(src, dst, send, recv, tile, group):
    return pltpu.make_async_remote_copy(
        src_ref=src, dst_ref=dst, send_sem=send, recv_sem=recv,
        device_id={"tile": tile, "group": group}, device_id_type=MESH,
    )


class AllReduce:
    def __init__(self, plan, part, pair, mine, came, full, sems):
        self.p, self.part, self.pair, self.mine = plan, part, pair, mine
        self.came, self.full, self.sems = came, full, sems

    def pair_copy(self):
        p = self.p
        return remote(self.part.at[1 - p.h, p.s], self.pair, self.sems[0].at[0],
                      self.sems[1].at[0], p.partner, p.g)

    def spread_copy(self, d):
        p = self.p
        to = lax.rem(p.k + d, p.H)
        return remote(self.mine.at[to], self.came.at[d - 1], self.sems[2].at[d - 1],
                      self.sems[3].at[d - 1], 2 * to + p.h, p.g)

    def collect_copy(self, dg, dk, arriving):
        p = self.p
        n = dg * p.H + dk
        sign = -1 if arriving else 1
        k = lax.rem(p.k + sign * dk + p.H, p.H)
        s = lax.rem(p.s + sign * dg + p.gs, p.gs)
        slot = self.full.at[p.h, s, k] if arriving else self.full.at[p.h, p.s, p.k]
        return remote(slot, slot, self.sems[4].at[n], self.sems[5].at[n],
                      2 * k + p.h, p.g - p.s + s)

    def relay_copy(self, dg, dk, arriving):
        p = self.p
        n = dg * p.H + dk
        k = lax.rem(p.k - dk + p.H, p.H)
        s = lax.rem(p.s - dg + p.gs, p.gs)
        h = 1 - p.h if arriving else p.h
        slot = self.full.at[h, s, k]
        return remote(slot, slot, self.sems[6].at[n], self.sems[7].at[n], p.partner, p.g)

    def others(self):
        p = self.p
        return [(dg, dk) for dk in range(p.H) for dg in range(p.gs) if dg or dk]

    def put(self, channel, value):
        p = self.p
        self.part[:, :, :, channel] = value.reshape(2, p.gs, p.H, p.rows, value.shape[-1])

    def start_pair(self):
        self.pair_copy().start()

    def start_spread(self):
        p = self.p
        self.pair_copy().wait()
        self.mine[...] = self.part[p.h, p.s] + self.pair[...]
        for d in range(1, p.H):
            self.spread_copy(d).start()

    def start_collect(self):
        p = self.p
        total = self.mine[p.k]
        for d in range(1, p.H):
            self.spread_copy(d).wait()
            total = total + self.came[d - 1]
        self.full[p.h, p.s, p.k] = total
        for dg, dk in self.others():
            self.collect_copy(dg, dk, False).start()
        self.relay_copy(0, 0, False).start()

    def relay(self):
        for dg, dk in self.others():
            self.collect_copy(dg, dk, True).wait_recv()
            self.relay_copy(dg, dk, False).start()

    def finish(self):
        self.relay_copy(0, 0, True).wait_recv()
        self.relay_copy(0, 0, False).wait_send()
        for dg, dk in self.others():
            self.relay_copy(dg, dk, True).wait_recv()
            self.relay_copy(dg, dk, False).wait_send()
            self.collect_copy(dg, dk, False).wait_send()

    def get(self, channel):
        whole = self.full[:, :, :, channel]
        return whole.reshape(-1, whole.shape[-1])


class Plan:
    pass


def kernel(T, G, gs, row_in, column_in, live_in, obj, probe_in, amp, *args):
    tables_in, args = args[:4], args[4:]
    (obj_step, probe_step, scal_in, probe, *args) = args
    (a_head, a_tail, b_head, b_tail, load_sem, far), args = args[:6], args[6:]
    body(T, G, gs, (row_in, column_in, live_in), (obj, probe_in, amp, *tables_in),
         (probe, a_head, a_tail, b_head, b_tail), load_sem, far, scal_in, probe, a_head, a_tail,
         b_head, b_tail, obj_step, probe_step, *args)


def body(T, G, gs, scalars, inputs, loaded, load_sem, far, scal_in, probe, a_head, a_tail, b_head,
         b_tail, obj_step, probe_step, pad, amps, scal_all, win, terms, light_terms, acc, acc_light,
           edge, edge_light, grad_sum, *rest):
    t, g = lax.axis_index("tile"), lax.axis_index("group")
    obj, probe_in, amp, *tables_in = inputs
    R, W = obj.shape[1], probe.shape[1]
    B = obj.shape[2]
    rows = pad.shape[2]
    p = Plan()
    p.g, p.H, p.gs = g, T // 2, gs
    p.k, p.h = lax.div(t, 2), lax.rem(t, 2)
    p.partner = t + 1 - 2 * p.h
    p.s = lax.rem(g, gs)
    p.rows = W // 2 // (p.H * gs)
    light_red = AllReduce(p, *rest[0:5], rest[5:13])
    grad_red = AllReduce(p, *rest[13:18], rest[18:26])
    (own_s, own_r, side_s, side_r, amp_s, amp_r, scal_s, scal_r,
     edge_s, edge_r) = rest[26:36]

    own = pad.at[1, :, pl.ds(pl.multiple_of(g * R, 8), R)]
    loads = [pltpu.make_async_copy(src, dst, load_sem.at[i]) for i, (src, dst) in enumerate(
        [(obj, own), (amp.at[0], amps.at[g]), *zip((probe_in, *tables_in), loaded)])]
    for load in loads:
        load.start()
    barrier = pltpu.get_barrier_semaphore()
    count = 0
    for dt in range(T):
        for dg in range(G):
            if (dt or dg) and (dt == 0 or (dt % 2 == 0 and (G == gs or dg == 0))):
                pl.semaphore_signal(
                    barrier, inc=1,
                    device_id={"tile": lax.rem(t + dt, T), "group": lax.rem(g + dg, G)},
                    device_id_type=MESH)
                count += 1
    for to, there in ((t - 1, t > 0), (t + 1, t < T - 1)):
        @pl.when(there)
        def _():
            pl.semaphore_signal(barrier, inc=1, device_id={"tile": to, "group": g}, device_id_type=MESH)
    scal = scal_all
    line = lax.broadcasted_iota(jnp.int32, scal_in.shape, 0)
    scal_in[...] = jnp.where(line == 0, scalars[0][0], jnp.where(line == 1, scalars[1][0], scalars[2][0]))
    edges_here = (t > 0).astype(jnp.int32) + (t < T - 1).astype(jnp.int32)
    pl.semaphore_wait(barrier, count + edges_here)
    loads[0].wait()
    loads[1].wait()

    def span(group):
        return pl.ds(pl.multiple_of(group * R, 8), R)

    def to_peer(j, ch, arriving):
        peer = lax.rem(g + (G - j if arriving else j), G)
        slot = pad.at[1, ch, span(peer if arriving else g)]
        n = 2 * (j - 1) + ch
        return remote(slot, slot, own_s.at[n], own_r.at[n], t, peer)

    def to_side(j, ch, right, arriving):
        who = lax.rem(g + G - j, G)
        block = (0 if right else 2)
        dst = pad.at[block, ch, span(who)]
        src = pad.at[1, ch, span(who)]
        n = 4 * j + 2 * ch + int(right)
        return remote(dst if arriving else src, dst, side_s.at[n], side_r.at[n],
                      (t + 1 if right else t - 1) if not arriving else (t - 1 if right else t + 1), g)

    def amp_copy(j, arriving):
        peer = lax.rem(g + (G - j if arriving else j), G)
        slot = amps.at[peer if arriving else g]
        return remote(slot, slot, amp_s.at[j - 1], amp_r.at[j - 1], t, peer)

    def scal_copy(j, arriving):
        peer = lax.rem(g + (G - j if arriving else j), G)
        slot = scal.at[peer if arriving else g]
        return remote(slot if arriving else scal_in, slot, scal_s.at[j - 1], scal_r.at[j - 1], t, peer)

    def edge_copy(src, dst, right, base, arriving):
        n = base + int(right)
        side = dst.at[0 if right else 1]
        if arriving:
            return remote(side, side, edge_s.at[n], edge_r.at[n], t - 1 if right else t + 1, g)
        return remote(src.at[2 if right else 0], side, edge_s.at[n], edge_r.at[n],
                      t + 1 if right else t - 1, g)

    not_first, not_last = t > 0, t < T - 1

    for ch in range(2):
        for j in range(1, G):
            to_peer(j, ch, False).start()
    for ch in range(2):
        pl.when(not_first)(lambda: to_side(0, ch, False, False).start())
        pl.when(not_last)(lambda: to_side(0, ch, True, False).start())
    for j in range(1, G):
        scal_copy(j, False).start()
    for j in range(1, G):
        amp_copy(j, False).start()

    scal[g] = scal_in[...]

    @pl.when(t == 0)
    def _():
        pad[0] = jnp.zeros(pad.shape[1:], F32)
        edge[0] = jnp.zeros(edge.shape[1:], F32)
        edge_light[0] = jnp.zeros(edge_light.shape[1:], F32)

    @pl.when(t == T - 1)
    def _():
        pad[2] = jnp.zeros(pad.shape[1:], F32)
        edge[1] = jnp.zeros(edge.shape[1:], F32)
        edge_light[1] = jnp.zeros(edge_light.shape[1:], F32)

    spare = rows - W
    blocks = W // B
    terms[:, :, 0:spare] = jnp.zeros((2, blocks, spare, B), F32)
    terms[:, :, spare + W:] = jnp.zeros((2, blocks, spare, B), F32)
    light_terms[:, 0:spare] = jnp.zeros((blocks, spare, B), F32)
    light_terms[:, spare + W:] = jnp.zeros((blocks, spare, B), F32)

    def hold(ref, value):
        for b in range(blocks):
            ref[b, spare:spare + W] = value[:, b * B:(b + 1) * B]

    for load in loads[2:]:
        load.wait()
    probe_light = probe[0] * probe[0] + probe[1] * probe[1]
    hold(light_terms, probe_light)
    light_max = jnp.max(probe_light) + 1e-06

    for ch in range(2):
        for j in range(1, G):
            to_peer(j, ch, True).wait_recv()
            pl.when(not_first)(lambda: to_side(j, ch, False, False).start())
            pl.when(not_last)(lambda: to_side(j, ch, True, False).start())
    for j in range(1, G):
        scal_copy(j, True).wait_recv()
    for j in range(G):
        for ch in range(2):
            pl.when(not_last)(lambda: to_side(j, ch, False, True).wait_recv())
            pl.when(not_first)(lambda: to_side(j, ch, True, True).wait_recv())

    def numbers(k):
        return scal[k, 0, 0], scal[k, 1, 0], scal[k, 2, 0].astype(F32)

    def placed(ref, row, column):
        first = g * R + spare - row
        pieces = [ref[b, pl.ds(first, R), :] for b in range(blocks)]
        wide = jnp.concatenate(pieces + [jnp.zeros((R, 3 * B - W), F32)], axis=1)
        return pltpu.roll(wide, column, 1)

    acc[...] = jnp.zeros(acc.shape, F32)
    acc_light[...] = jnp.zeros(acc_light.shape, F32)
    grad_sum[...] = jnp.zeros(grad_sum.shape, F32)

    def look(j, light):
        k = lax.rem(g + j, G)
        row, column, weight = numbers(k)
        for ch in range(2):
            wide = jnp.concatenate([pad[b, ch, pl.ds(row, W), :] for b in range(3)], axis=1)
            win[k, ch] = pltpu.roll(wide, lax.rem(3 * B - column, 3 * B), 1)[:, 0:W]
        spread = weight * placed(light_terms, row, column)
        for b in range(3):
            acc_light[b] += spread[:, b * B:(b + 1) * B]
        return light + weight * (win[k, 0] * win[k, 0] + win[k, 1] * win[k, 1])

    light = lax.fori_loop(0, G, look, jnp.zeros((W, W), F32))
    light_red.put(0, light)
    light_red.start_pair()
    pl.when(not_first)(lambda: edge_copy(acc_light, edge_light, False, 0, False).start())
    pl.when(not_last)(lambda: edge_copy(acc_light, edge_light, True, 0, False).start())

    def forth(k):
        wr, wi = win[k, 0], win[k, 1]
        pr, pi = probe[0], probe[1]
        x = jnp.concatenate([pr * wr - pi * wi, pr * wi + pi * wr], axis=0)
        y = table_left(a_head[...], a_tail[...], x)
        z = table_right(jnp.concatenate([y[:W], y[W:]], axis=1), b_head[...], b_tail[...])
        zr, zi = z[:, :W], z[:, W:]
        factor = 1.0 - amps[k] * lax.rsqrt(jnp.maximum(zr * zr + zi * zi, 0.0625))
        far[0:W], far[W:] = zr * factor, zi * factor

    def back(k):
        row, column, weight = numbers(k)
        wr, wi = win[k, 0], win[k, 1]
        pr, pi = probe[0], probe[1]
        x = far[...]
        y = table_left(b_head[...], b_tail[...], x)
        z = table_right(jnp.concatenate([y[:W], y[W:]], axis=1), a_head[...], a_tail[...])
        mr, mi = z[:, :W] * weight, z[:, W:] * weight
        hold(terms.at[0], pr * mr + pi * mi)
        hold(terms.at[1], pr * mi - pi * mr)
        grad_sum[0] += wr * mr + wi * mi
        grad_sum[1] += wr * mi - wi * mr
        for ch in range(2):
            spread = placed(terms.at[ch], row, column)
            for b in range(3):
                acc[b, ch] += spread[:, b * B:(b + 1) * B]

    forth(g)
    light_red.start_spread()
    back(g)
    for j in range(1, G):
        amp_copy(j, True).wait_recv()

    def both(j):
        back(lax.rem(g + j, G))
        forth(lax.rem(g + j + 1, G))

    if G > 1:
        forth(lax.rem(g + 1, G))
        light_red.start_collect()
        pl.loop(1, G - 1)(both)
        back(lax.rem(g + G - 1, G))
    else:
        light_red.start_collect()

    for ch in range(2):
        grad_red.put(ch, grad_sum[ch])
    grad_red.start_pair()
    pl.when(not_first)(lambda: edge_copy(acc, edge, False, 2, False).start())
    pl.when(not_last)(lambda: edge_copy(acc, edge, True, 2, False).start())
    grad_red.start_spread()
    light_red.relay()
    grad_red.start_collect()

    for src, dst, base in ((acc_light, edge_light, 0), (acc, edge, 2)):
        pl.when(not_last)(lambda: edge_copy(src, dst, False, base, True).wait_recv())
        pl.when(not_first)(lambda: edge_copy(src, dst, True, base, True).wait_recv())
    below = 1.0 / (acc_light[1] + edge_light[0] + edge_light[1] + 0.25 * light_max)
    for ch in range(2):
        obj_step[ch] = (acc[1, ch] + edge[0, ch] + edge[1, ch]) * below
    light_red.finish()
    light = light_red.get(0)
    below = 1.0 / (light + 0.25 * jnp.mean(light) + 1e-05)
    grad_red.relay()
    grad_red.finish()
    for ch in range(2):
        probe_step[ch] = grad_red.get(ch) * below

    for j in range(1, G):
        for ch in range(2):
            to_peer(j, ch, False).wait_send()
        amp_copy(j, False).wait_send()
        scal_copy(j, False).wait_send()
    for j in range(G):
        for ch in range(2):
            pl.when(not_first)(lambda: to_side(j, ch, False, False).wait_send())
            pl.when(not_last)(lambda: to_side(j, ch, True, False).wait_send())
    for src, dst, base in ((acc_light, edge_light, 0), (acc, edge, 2)):
        pl.when(not_first)(lambda: edge_copy(src, dst, False, base, False).wait_send())
        pl.when(not_last)(lambda: edge_copy(src, dst, True, base, False).wait_send())


def local(T, G, object_field, probe_field, amplitudes, row_start, column_start, live_slots):
    R, B = object_field.shape[1:]
    W = probe_field.shape[1]
    rows = R * G
    H = T // 2
    gs = max(n for n in range(1, G + 1) if G % n == 0 and n * H * 8 <= W // 2)
    chunk = W // 2 // (H * gs)
    head, tail = dft_tables(W)
    spare = rows - W
    dma = lambda n: pltpu.SemaphoreType.DMA((max(n, 1),))

    def reduce_scratch(channels):
        return [
            pltpu.VMEM((2, gs, H, channels, chunk, W), F32),
            pltpu.VMEM((H, channels, chunk, W), F32),
            pltpu.VMEM((H, channels, chunk, W), F32),
            pltpu.VMEM((H - 1, channels, chunk, W), F32),
            pltpu.VMEM((2, gs, H, channels, chunk, W), F32),
            dma(1), dma(1), dma(H - 1), dma(H - 1), dma(gs * H), dma(gs * H), dma(gs * H), dma(gs * H),
        ]

    vmem_limit = 67043328 - 4 * (object_field.size + probe_field.size) - 65536
    smem = pl.BlockSpec(memory_space=pltpu.SMEM)
    hbm = pl.BlockSpec(memory_space=pltpu.HBM)
    vmem = pl.BlockSpec(memory_space=pltpu.VMEM)
    obj_step, probe_step = pl.pallas_call(
        functools.partial(kernel, T, G, gs),
        out_shape=(pltpu.VMEM(object_field.shape, F32), pltpu.VMEM(probe_field.shape, F32)),
        in_specs=[smem] * 3 + [hbm] * 7,
        out_specs=(vmem, vmem),
        scratch_shapes=[
            pltpu.VMEM((8, 128), jnp.int32),
            pltpu.VMEM(probe_field.shape, F32),
            *[pltpu.VMEM(head.shape, BF16)] * 4,
            dma(7),
            pltpu.VMEM((2 * W, W), F32),
            pltpu.VMEM((3, 2, rows, B), F32),
            pltpu.VMEM((G, W, W), F32),
            pltpu.VMEM((G, 8, 128), jnp.int32),
            pltpu.VMEM((G, 2, W, W), F32),
            pltpu.VMEM((2, W // B, W + 2 * spare, B), F32),
            pltpu.VMEM((W // B, W + 2 * spare, B), F32),
            pltpu.VMEM((3, 2, R, B), F32),
            pltpu.VMEM((3, R, B), F32),
            pltpu.VMEM((2, 2, R, B), F32),
            pltpu.VMEM((2, R, B), F32),
            pltpu.VMEM((2, W, W), F32),
            *reduce_scratch(1),
            *reduce_scratch(2),
            dma(2 * G - 2), dma(2 * G - 2), dma(4 * G), dma(4 * G), dma(G - 1), dma(G - 1),
            dma(G - 1), dma(G - 1), dma(4), dma(4),
        ],
        compiler_params=pltpu.CompilerParams(
            collective_id=0, has_side_effects=True, vmem_limit_bytes=vmem_limit),
    )(row_start, column_start, live_slots, object_field, probe_field, amplitudes, head, tail,
      head.T, tail.T)
    return object_field - obj_step, probe_field - probe_step


def solution(mesh):
    return jax.shard_map(
        functools.partial(local, mesh.shape["tile"], mesh.shape["group"]),
        mesh=mesh,
        in_specs=(
            P(None, "group", "tile"),
            P(),
            P(("tile", "group"), None, None),
            P(("tile", "group")),
            P(("tile", "group")),
            P(("tile", "group")),
        ),
        out_specs=(P(None, "group", "tile"), P()),
        check_vma=False,
    )
```

```python
import functools
import math

import jax
import jax.numpy as jnp
import numpy as np
from jax import lax
from jax.experimental import pallas as pl
from jax.experimental.pallas import tpu as pltpu
from jax.sharding import PartitionSpec as P

MESH = pl.DeviceIdType.MESH
F32 = jnp.float32
BF16 = jnp.bfloat16


def dft_tables(length):
    k = np.arange(length)
    angles = 2.0 * math.pi / length * (np.outer(k, k) % length)
    cos, sin = np.cos(angles) / math.sqrt(length), np.sin(angles) / math.sqrt(length)
    full = np.block([[cos, sin], [-sin, cos]]).astype(np.float32)
    head = full.astype(BF16)
    tail = (full - head.astype(np.float32)).astype(BF16)
    return head, tail


def split(x):
    head = x.astype(BF16)
    return head, (x - head.astype(F32)).astype(BF16)


def mm(a, b):
    return jnp.dot(a, b, preferred_element_type=F32)


def table_left(head, tail, x):
    xh, xl = split(x)
    return mm(head, xh) + (mm(head, xl) + mm(tail, xh))


def table_right(x, head, tail):
    xh, xl = split(x)
    return mm(xh, head) + (mm(xl, head) + mm(xh, tail))


def remote(src, dst, send, recv, tile, group):
    return pltpu.make_async_remote_copy(
        src_ref=src, dst_ref=dst, send_sem=send, recv_sem=recv,
        device_id={"tile": tile, "group": group}, device_id_type=MESH,
    )


class AllReduce:
    def __init__(self, plan, part, pair, mine, came, full, sems):
        self.p, self.part, self.pair, self.mine = plan, part, pair, mine
        self.came, self.full, self.sems = came, full, sems

    def pair_copy(self):
        p = self.p
        return remote(self.part.at[1 - p.h, p.s], self.pair, self.sems[0].at[0],
                      self.sems[1].at[0], p.partner, p.g)

    def spread_copy(self, d):
        p = self.p
        to = lax.rem(p.k + d, p.H)
        return remote(self.mine.at[to], self.came.at[d - 1], self.sems[2].at[d - 1],
                      self.sems[3].at[d - 1], 2 * to + p.h, p.g)

    def collect_copy(self, dg, dk, arriving):
        p = self.p
        n = dg * p.H + dk
        sign = -1 if arriving else 1
        if dg == 0:
            k = lax.rem(p.k + sign * dk + p.H, p.H)
            slot = self.full.at[p.h, p.s, k if arriving else p.k]
            to, group = 2 * k + p.h, p.g
        else:
            s = lax.rem(p.s + sign * dg + p.gs, p.gs)
            slot = self.full.at[p.h, s if arriving else p.s, lax.rem(p.k - dk + p.H, p.H)]
            to, group = 2 * p.k + p.h, p.g - p.s + s
        return remote(slot, slot, self.sems[4].at[n], self.sems[5].at[n], to, group)

    def relay_copy(self, dg, dk, arriving):
        p = self.p
        n = dg * p.H + dk
        k = lax.rem(p.k - dk + p.H, p.H)
        s = lax.rem(p.s - dg + p.gs, p.gs)
        h = 1 - p.h if arriving else p.h
        slot = self.full.at[h, s, k]
        return remote(slot, slot, self.sems[6].at[n], self.sems[7].at[n], p.partner, p.g)

    def others(self):
        p = self.p
        return [(dg, dk) for dk in range(p.H) for dg in range(p.gs) if dg or dk]

    def put(self, channel, value):
        p = self.p
        self.part[:, :, :, channel] = value.reshape(2, p.gs, p.H, p.rows, value.shape[-1])

    def start_pair(self):
        self.pair_copy().start()

    def start_spread(self):
        p = self.p
        self.pair_copy().wait()
        self.mine[...] = self.part[p.h, p.s] + self.pair[...]
        for d in range(1, p.H):
            self.spread_copy(d).start()

    def start_collect(self):
        p = self.p
        total = self.mine[p.k]
        for d in range(1, p.H):
            self.spread_copy(d).wait()
            total = total + self.came[d - 1]
        self.full[p.h, p.s, p.k] = total
        for dk in range(1, p.H):
            self.collect_copy(0, dk, False).start()
        for dg in range(1, p.gs):
            self.collect_copy(dg, 0, False).start()
        self.relay_copy(0, 0, False).start()

    def relay(self):
        p = self.p
        for dk in range(p.H):
            if dk > 0:
                self.collect_copy(0, dk, True).wait_recv()
                for dg in range(1, p.gs):
                    self.collect_copy(dg, dk, False).start()
                self.relay_copy(0, dk, False).start()
        for dk in range(p.H):
            for dg in range(1, p.gs):
                self.collect_copy(dg, dk, True).wait_recv()
                self.relay_copy(dg, dk, False).start()

    def finish(self):
        self.relay_copy(0, 0, True).wait_recv()
        self.relay_copy(0, 0, False).wait_send()
        for dg, dk in self.others():
            self.relay_copy(dg, dk, True).wait_recv()
            self.relay_copy(dg, dk, False).wait_send()
            self.collect_copy(dg, dk, False).wait_send()

    def get(self, channel):
        whole = self.full[:, :, :, channel]
        return whole.reshape(-1, whole.shape[-1])


class Plan:
    pass


def kernel(T, G, gs, row_in, column_in, live_in, obj, probe_in, amp, *args):
    tables_in, args = args[:4], args[4:]
    (new_obj, new_probe, scal_in, probe, *args) = args
    (a_head, a_tail, b_head, b_tail, load_sem, far), args = args[:6], args[6:]
    body(T, G, gs, (row_in, column_in, live_in), (obj, probe_in, amp, *tables_in),
         (probe, a_head, a_tail, b_head, b_tail), load_sem, far, scal_in, probe, a_head, a_tail,
         b_head, b_tail, new_obj, new_probe, *args)


def body(T, G, gs, scalars, inputs, loaded, load_sem, far, scal_in, probe, a_head, a_tail, b_head,
         b_tail, new_obj, new_probe, pad, amps, scal_all, win, terms, light_terms, acc, acc_light,
           edge, edge_light, grad_sum, *rest):
    t, g = lax.axis_index("tile"), lax.axis_index("group")
    obj, probe_in, amp, *tables_in = inputs
    R, W = obj.shape[1], probe.shape[1]
    B = obj.shape[2]
    rows = pad.shape[2]
    p = Plan()
    p.g, p.H, p.gs = g, T // 2, gs
    p.k, p.h = lax.div(t, 2), lax.rem(t, 2)
    p.partner = t + 1 - 2 * p.h
    p.s = lax.rem(g, gs)
    p.rows = W // 2 // (p.H * gs)
    light_red = AllReduce(p, *rest[0:5], rest[5:13])
    grad_red = AllReduce(p, *rest[13:18], rest[18:26])
    (own_s, own_r, side_s, side_r, amp_s, amp_r, scal_s, scal_r,
     edge_s, edge_r) = rest[26:36]

    own = pad.at[1, :, pl.ds(pl.multiple_of(g * R, 8), R)]
    loads = [pltpu.make_async_copy(src, dst, load_sem.at[i]) for i, (src, dst) in enumerate(
        [(obj, own), (amp.at[0], amps.at[g]), *zip((probe_in, *tables_in), loaded)])]
    for load in loads:
        load.start()
    barrier = pltpu.get_barrier_semaphore()
    count = 0
    for dt in range(T):
        for dg in range(G):
            if (dt or dg) and (dt == 0 or (dt % 2 == 0 and dg == 0)):
                pl.semaphore_signal(
                    barrier, inc=1,
                    device_id={"tile": lax.rem(t + dt, T), "group": lax.rem(g + dg, G)},
                    device_id_type=MESH)
                count += 1
    for to, there in ((t - 1, t > 0), (t + 1, t < T - 1)):
        @pl.when(there)
        def _():
            pl.semaphore_signal(barrier, inc=1, device_id={"tile": to, "group": g}, device_id_type=MESH)
    scal = scal_all
    line = lax.broadcasted_iota(jnp.int32, scal_in.shape, 0)
    scal_in[...] = jnp.where(line == 0, scalars[0][0], jnp.where(line == 1, scalars[1][0], scalars[2][0]))
    edges_here = (t > 0).astype(jnp.int32) + (t < T - 1).astype(jnp.int32)
    pl.semaphore_wait(barrier, count + edges_here)
    loads[0].wait()
    loads[1].wait()

    def span(group):
        return pl.ds(pl.multiple_of(group * R, 8), R)

    def to_peer(j, ch, arriving):
        peer = lax.rem(g + (G - j if arriving else j), G)
        slot = pad.at[1, ch, span(peer if arriving else g)]
        n = 2 * (j - 1) + ch
        return remote(slot, slot, own_s.at[n], own_r.at[n], t, peer)

    def to_side(j, ch, right, arriving):
        who = lax.rem(g + G - j, G)
        block = (0 if right else 2)
        dst = pad.at[block, ch, span(who)]
        src = pad.at[1, ch, span(who)]
        n = 4 * j + 2 * ch + int(right)
        return remote(dst if arriving else src, dst, side_s.at[n], side_r.at[n],
                      (t + 1 if right else t - 1) if not arriving else (t - 1 if right else t + 1), g)

    def amp_copy(j, arriving):
        peer = lax.rem(g + (G - j if arriving else j), G)
        slot = amps.at[peer if arriving else g]
        return remote(slot, slot, amp_s.at[j - 1], amp_r.at[j - 1], t, peer)

    def scal_copy(j, arriving):
        peer = lax.rem(g + (G - j if arriving else j), G)
        slot = scal.at[peer if arriving else g]
        return remote(slot if arriving else scal_in, slot, scal_s.at[j - 1], scal_r.at[j - 1], t, peer)

    def edge_copy(src, dst, right, base, arriving):
        n = base + int(right)
        side = dst.at[0 if right else 1]
        if arriving:
            return remote(side, side, edge_s.at[n], edge_r.at[n], t - 1 if right else t + 1, g)
        return remote(src.at[2 if right else 0], side, edge_s.at[n], edge_r.at[n],
                      t + 1 if right else t - 1, g)

    not_first, not_last = t > 0, t < T - 1

    for ch in range(2):
        for j in range(1, G):
            to_peer(j, ch, False).start()
    for ch in range(2):
        pl.when(not_first)(lambda: to_side(0, ch, False, False).start())
        pl.when(not_last)(lambda: to_side(0, ch, True, False).start())
    for j in range(1, G):
        scal_copy(j, False).start()
    for j in range(1, G):
        amp_copy(j, False).start()

    scal[g] = scal_in[...]

    @pl.when(t == 0)
    def _():
        pad[0] = jnp.zeros(pad.shape[1:], F32)
        edge[0] = jnp.zeros(edge.shape[1:], F32)
        edge_light[0] = jnp.zeros(edge_light.shape[1:], F32)

    @pl.when(t == T - 1)
    def _():
        pad[2] = jnp.zeros(pad.shape[1:], F32)
        edge[1] = jnp.zeros(edge.shape[1:], F32)
        edge_light[1] = jnp.zeros(edge_light.shape[1:], F32)

    spare = rows - W
    blocks = W // B
    terms[:, :, 0:spare] = jnp.zeros((2, blocks, spare, B), F32)
    terms[:, :, spare + W:] = jnp.zeros((2, blocks, spare, B), F32)
    light_terms[:, 0:spare] = jnp.zeros((blocks, spare, B), F32)
    light_terms[:, spare + W:] = jnp.zeros((blocks, spare, B), F32)

    def hold(ref, value):
        for b in range(blocks):
            ref[b, spare:spare + W] = value[:, b * B:(b + 1) * B]

    for load in loads[2:]:
        load.wait()
    probe_light = probe[0] * probe[0] + probe[1] * probe[1]
    hold(light_terms, probe_light)
    light_max = jnp.max(probe_light) + 1e-06

    for ch in range(2):
        for j in range(1, G):
            to_peer(j, ch, True).wait_recv()
            pl.when(not_first)(lambda: to_side(j, ch, False, False).start())
            pl.when(not_last)(lambda: to_side(j, ch, True, False).start())
    for j in range(1, G):
        scal_copy(j, True).wait_recv()
    for j in range(G):
        for ch in range(2):
            pl.when(not_last)(lambda: to_side(j, ch, False, True).wait_recv())
            pl.when(not_first)(lambda: to_side(j, ch, True, True).wait_recv())

    def numbers(k):
        return scal[k, 0, 0], scal[k, 1, 0], scal[k, 2, 0].astype(F32)

    def placed(ref, row, column):
        first = g * R + spare - row
        pieces = [ref[b, pl.ds(first, R), :] for b in range(blocks)]
        wide = jnp.concatenate(pieces + [jnp.zeros((R, 3 * B - W), F32)], axis=1)
        return pltpu.roll(wide, column, 1)

    acc[...] = jnp.zeros(acc.shape, F32)
    acc_light[...] = jnp.zeros(acc_light.shape, F32)
    grad_sum[...] = jnp.zeros(grad_sum.shape, F32)

    def look(j, light):
        k = lax.rem(g + j, G)
        row, column, weight = numbers(k)
        for ch in range(2):
            wide = jnp.concatenate([pad[b, ch, pl.ds(row, W), :] for b in range(3)], axis=1)
            win[k, ch] = pltpu.roll(wide, lax.rem(3 * B - column, 3 * B), 1)[:, 0:W]
        spread = weight * placed(light_terms, row, column)
        for b in range(3):
            acc_light[b] += spread[:, b * B:(b + 1) * B]
        return light + weight * (win[k, 0] * win[k, 0] + win[k, 1] * win[k, 1])

    light = lax.fori_loop(0, G, look, jnp.zeros((W, W), F32))
    light_red.put(0, light)
    light_red.start_pair()
    pl.when(not_first)(lambda: edge_copy(acc_light, edge_light, False, 0, False).start())
    pl.when(not_last)(lambda: edge_copy(acc_light, edge_light, True, 0, False).start())

    def forth(k):
        wr, wi = win[k, 0], win[k, 1]
        pr, pi = probe[0], probe[1]
        x = jnp.concatenate([pr * wr - pi * wi, pr * wi + pi * wr], axis=0)
        y = table_left(a_head[...], a_tail[...], x)
        z = table_right(jnp.concatenate([y[:W], y[W:]], axis=1), b_head[...], b_tail[...])
        zr, zi = z[:, :W], z[:, W:]
        factor = 1.0 - amps[k] * lax.rsqrt(jnp.maximum(zr * zr + zi * zi, 0.0625))
        far[0:W], far[W:] = zr * factor, zi * factor

    def back(k):
        row, column, weight = numbers(k)
        wr, wi = win[k, 0], win[k, 1]
        pr, pi = probe[0], probe[1]
        x = far[...]
        y = table_left(b_head[...], b_tail[...], x)
        z = table_right(jnp.concatenate([y[:W], y[W:]], axis=1), a_head[...], a_tail[...])
        mr, mi = z[:, :W] * weight, z[:, W:] * weight
        hold(terms.at[0], pr * mr + pi * mi)
        hold(terms.at[1], pr * mi - pi * mr)
        grad_sum[0] += wr * mr + wi * mi
        grad_sum[1] += wr * mi - wi * mr
        for ch in range(2):
            spread = placed(terms.at[ch], row, column)
            for b in range(3):
                acc[b, ch] += spread[:, b * B:(b + 1) * B]

    forth(g)
    light_red.start_spread()
    back(g)
    for j in range(1, G):
        amp_copy(j, True).wait_recv()

    def both(j):
        back(lax.rem(g + j, G))
        forth(lax.rem(g + j + 1, G))

    if G > 1:
        forth(lax.rem(g + 1, G))
        light_red.start_collect()
        pl.loop(1, G - 1)(both)
        back(lax.rem(g + G - 1, G))
    else:
        light_red.start_collect()

    for ch in range(2):
        grad_red.put(ch, grad_sum[ch])
    grad_red.start_pair()
    pl.when(not_first)(lambda: edge_copy(acc, edge, False, 2, False).start())
    pl.when(not_last)(lambda: edge_copy(acc, edge, True, 2, False).start())
    grad_red.start_spread()
    light_red.relay()
    grad_red.start_collect()

    for src, dst, base in ((acc_light, edge_light, 0), (acc, edge, 2)):
        pl.when(not_last)(lambda: edge_copy(src, dst, False, base, True).wait_recv())
        pl.when(not_first)(lambda: edge_copy(src, dst, True, base, True).wait_recv())
    below = 1.0 / (acc_light[1] + edge_light[0] + edge_light[1] + 0.25 * light_max)
    for ch in range(2):
        new_obj[ch] = own[ch] - (acc[1, ch] + edge[0, ch] + edge[1, ch]) * below
    light_red.finish()
    light = light_red.get(0)
    below = 1.0 / (light + 0.25 * jnp.mean(light) + 1e-05)
    grad_red.relay()
    grad_red.finish()
    for ch in range(2):
        new_probe[ch] = probe[ch] - grad_red.get(ch) * below

    for j in range(1, G):
        for ch in range(2):
            to_peer(j, ch, False).wait_send()
        amp_copy(j, False).wait_send()
        scal_copy(j, False).wait_send()
    for j in range(G):
        for ch in range(2):
            pl.when(not_first)(lambda: to_side(j, ch, False, False).wait_send())
            pl.when(not_last)(lambda: to_side(j, ch, True, False).wait_send())
    for src, dst, base in ((acc_light, edge_light, 0), (acc, edge, 2)):
        pl.when(not_first)(lambda: edge_copy(src, dst, False, base, False).wait_send())
        pl.when(not_last)(lambda: edge_copy(src, dst, True, base, False).wait_send())


def put(obj, probe, obj_out, probe_out, sems):
    copies = [pltpu.make_async_copy(obj, obj_out, sems.at[0]),
              pltpu.make_async_copy(probe, probe_out, sems.at[1])]
    for copy in copies:
        copy.start()
    for copy in copies:
        copy.wait()


def local(T, G, object_field, probe_field, amplitudes, row_start, column_start, live_slots):
    R, B = object_field.shape[1:]
    W = probe_field.shape[1]
    rows = R * G
    H = T // 2
    gs = max(n for n in range(1, G + 1) if G % n == 0 and n * H * 8 <= W // 2)
    chunk = W // 2 // (H * gs)
    head, tail = dft_tables(W)
    spare = rows - W
    dma = lambda n: pltpu.SemaphoreType.DMA((max(n, 1),))

    def reduce_scratch(channels):
        return [
            pltpu.VMEM((2, gs, H, channels, chunk, W), F32),
            pltpu.VMEM((H, channels, chunk, W), F32),
            pltpu.VMEM((H, channels, chunk, W), F32),
            pltpu.VMEM((H - 1, channels, chunk, W), F32),
            pltpu.VMEM((2, gs, H, channels, chunk, W), F32),
            dma(1), dma(1), dma(H - 1), dma(H - 1), dma(gs * H), dma(gs * H), dma(gs * H), dma(gs * H),
        ]

    vmem_limit = 67043328 - 4 * (object_field.size + probe_field.size) - 65536
    smem = pl.BlockSpec(memory_space=pltpu.SMEM)
    hbm = pl.BlockSpec(memory_space=pltpu.HBM)
    vmem = pl.BlockSpec(memory_space=pltpu.VMEM)
    new_obj, new_probe = pl.pallas_call(
        functools.partial(kernel, T, G, gs),
        out_shape=(pltpu.VMEM(object_field.shape, F32), pltpu.VMEM(probe_field.shape, F32)),
        in_specs=[smem] * 3 + [hbm] * 7,
        out_specs=(vmem, vmem),
        scratch_shapes=[
            pltpu.VMEM((8, 128), jnp.int32),
            pltpu.VMEM(probe_field.shape, F32),
            *[pltpu.VMEM(head.shape, BF16)] * 4,
            dma(7),
            pltpu.VMEM((2 * W, W), F32),
            pltpu.VMEM((3, 2, rows, B), F32),
            pltpu.VMEM((G, W, W), F32),
            pltpu.VMEM((G, 8, 128), jnp.int32),
            pltpu.VMEM((G, 2, W, W), F32),
            pltpu.VMEM((2, W // B, W + 2 * spare, B), F32),
            pltpu.VMEM((W // B, W + 2 * spare, B), F32),
            pltpu.VMEM((3, 2, R, B), F32),
            pltpu.VMEM((3, R, B), F32),
            pltpu.VMEM((2, 2, R, B), F32),
            pltpu.VMEM((2, R, B), F32),
            pltpu.VMEM((2, W, W), F32),
            *reduce_scratch(1),
            *reduce_scratch(2),
            dma(2 * G - 2), dma(2 * G - 2), dma(4 * G), dma(4 * G), dma(G - 1), dma(G - 1),
            dma(G - 1), dma(G - 1), dma(4), dma(4),
        ],
        compiler_params=pltpu.CompilerParams(
            collective_id=0, has_side_effects=True, vmem_limit_bytes=vmem_limit),
    )(row_start, column_start, live_slots, object_field, probe_field, amplitudes, head, tail,
      head.T, tail.T)
    anywhere = pl.BlockSpec(memory_space=pl.ANY)
    return pl.pallas_call(
        put,
        out_shape=(jax.ShapeDtypeStruct(object_field.shape, F32),
                   jax.ShapeDtypeStruct(probe_field.shape, F32)),
        in_specs=[vmem] * 2,
        out_specs=(anywhere, anywhere),
        scratch_shapes=[dma(2)],
        compiler_params=pltpu.CompilerParams(vmem_limit_bytes=1024 * 1024),
    )(new_obj, new_probe)


def solution(mesh):
    return jax.shard_map(
        functools.partial(local, mesh.shape["tile"], mesh.shape["group"]),
        mesh=mesh,
        in_specs=(
            P(None, "group", "tile"),
            P(),
            P(("tile", "group"), None, None),
            P(("tile", "group")),
            P(("tile", "group")),
            P(("tile", "group")),
        ),
        out_specs=(P(None, "group", "tile"), P()),
        check_vma=False,
    )
```

```python
import functools
import math

import jax
import jax.numpy as jnp
import numpy as np
from jax import lax
from jax.experimental import pallas as pl
from jax.experimental.pallas import tpu as pltpu
from jax.sharding import PartitionSpec as P

MESH = pl.DeviceIdType.MESH
F32 = jnp.float32
BF16 = jnp.bfloat16


def dft_tables(length):
    k = np.arange(length)
    angles = 2.0 * math.pi / length * (np.outer(k, k) % length)
    cos, sin = np.cos(angles) / math.sqrt(length), np.sin(angles) / math.sqrt(length)
    full = np.block([[cos, sin], [-sin, cos]]).astype(np.float32)
    head = full.astype(BF16)
    tail = (full - head.astype(np.float32)).astype(BF16)
    return head, tail


def split(x):
    head = x.astype(BF16)
    return head, (x - head.astype(F32)).astype(BF16)


def mm(a, b):
    return jnp.dot(a, b, preferred_element_type=F32)


def table_left(head, tail, x):
    xh, xl = split(x)
    return mm(head, xh) + (mm(head, xl) + mm(tail, xh))


def table_right(x, head, tail):
    xh, xl = split(x)
    return mm(xh, head) + (mm(xl, head) + mm(xh, tail))


def remote(src, dst, send, recv, tile, group):
    return pltpu.make_async_remote_copy(
        src_ref=src, dst_ref=dst, send_sem=send, recv_sem=recv,
        device_id={"tile": tile, "group": group}, device_id_type=MESH,
    )


class AllReduce:
    def __init__(self, plan, part, pair, mine, came, full, sems):
        self.p, self.part, self.pair, self.mine = plan, part, pair, mine
        self.came, self.full, self.sems = came, full, sems

    def pair_copy(self):
        p = self.p
        return remote(self.part.at[1 - p.h, p.s], self.pair, self.sems[0].at[0],
                      self.sems[1].at[0], p.partner, p.g)

    def spread_copy(self, d):
        p = self.p
        to = lax.rem(p.k + d, p.H)
        return remote(self.mine.at[to], self.came.at[d - 1], self.sems[2].at[d - 1],
                      self.sems[3].at[d - 1], 2 * to + p.h, p.g)

    def collect_copy(self, dg, dk, arriving):
        p = self.p
        n = dg * p.H + dk
        sign = -1 if arriving else 1
        if dg == 0:
            k = lax.rem(p.k + sign * dk + p.H, p.H)
            slot = self.full.at[p.h, p.s, k if arriving else p.k]
            to, group = 2 * k + p.h, p.g
        else:
            s = lax.rem(p.s + sign * dg + p.gs, p.gs)
            slot = self.full.at[p.h, s if arriving else p.s, lax.rem(p.k - dk + p.H, p.H)]
            to, group = 2 * p.k + p.h, p.g - p.s + s
        return remote(slot, slot, self.sems[4].at[n], self.sems[5].at[n], to, group)

    def relay_copy(self, dg, dk, arriving):
        p = self.p
        n = dg * p.H + dk
        k = lax.rem(p.k - dk + p.H, p.H)
        s = lax.rem(p.s - dg + p.gs, p.gs)
        h = 1 - p.h if arriving else p.h
        slot = self.full.at[h, s, k]
        return remote(slot, slot, self.sems[6].at[n], self.sems[7].at[n], p.partner, p.g)

    def others(self):
        p = self.p
        return [(dg, dk) for dk in range(p.H) for dg in range(p.gs) if dg or dk]

    def put(self, channel, value):
        p = self.p
        self.part[:, :, :, channel] = value.reshape(2, p.gs, p.H, p.rows, value.shape[-1])

    def start_pair(self):
        self.pair_copy().start()

    def start_spread(self):
        p = self.p
        self.pair_copy().wait()
        self.mine[...] = self.part[p.h, p.s] + self.pair[...]
        for d in range(1, p.H):
            self.spread_copy(d).start()

    def start_collect(self):
        p = self.p
        total = self.mine[p.k]
        for d in range(1, p.H):
            self.spread_copy(d).wait()
            total = total + self.came[d - 1]
        self.full[p.h, p.s, p.k] = total
        for dk in range(1, p.H):
            self.collect_copy(0, dk, False).start()
        for dg in range(1, p.gs):
            self.collect_copy(dg, 0, False).start()
        self.relay_copy(0, 0, False).start()

    def relay(self):
        p = self.p
        for dk in range(p.H):
            if dk > 0:
                self.collect_copy(0, dk, True).wait_recv()
                for dg in range(1, p.gs):
                    self.collect_copy(dg, dk, False).start()
                self.relay_copy(0, dk, False).start()
        for dk in range(p.H):
            for dg in range(1, p.gs):
                self.collect_copy(dg, dk, True).wait_recv()
                self.relay_copy(dg, dk, False).start()

    def finish(self):
        self.relay_copy(0, 0, True).wait_recv()
        self.relay_copy(0, 0, False).wait_send()
        for dg, dk in self.others():
            self.relay_copy(dg, dk, True).wait_recv()
            self.relay_copy(dg, dk, False).wait_send()
            self.collect_copy(dg, dk, False).wait_send()

    def get(self, channel):
        whole = self.full[:, :, :, channel]
        return whole.reshape(-1, whole.shape[-1])


class Plan:
    pass


def kernel(T, G, gs, row_in, column_in, live_in, obj, probe_in, amp, *args):
    tables_in, args = args[:4], args[4:]
    (new_obj, new_probe, scal_in, probe, *args) = args
    (a_head, a_tail, b_head, b_tail, load_sem, far), args = args[:6], args[6:]
    body(T, G, gs, (row_in, column_in, live_in), (obj, probe_in, amp, *tables_in),
         (probe, a_head, a_tail, b_head, b_tail), load_sem, far, scal_in, probe, a_head, a_tail,
         b_head, b_tail, new_obj, new_probe, *args)


def body(T, G, gs, scalars, inputs, loaded, load_sem, far, scal_in, probe, a_head, a_tail, b_head,
         b_tail, new_obj, new_probe, pad, amps, scal_all, win, terms, light_terms, acc, acc_light,
           edge, edge_light, grad_sum, *rest):
    t, g = lax.axis_index("tile"), lax.axis_index("group")
    obj, probe_in, amp, *tables_in = inputs
    R, W = obj.shape[1], probe.shape[1]
    B = obj.shape[2]
    rows = pad.shape[2]
    p = Plan()
    p.g, p.H, p.gs = g, T // 2, gs
    p.k, p.h = lax.div(t, 2), lax.rem(t, 2)
    p.partner = t + 1 - 2 * p.h
    p.s = lax.rem(g, gs)
    p.rows = W // 2 // (p.H * gs)
    light_red = AllReduce(p, *rest[0:5], rest[5:13])
    grad_red = AllReduce(p, *rest[13:18], rest[18:26])
    (own_s, own_r, side_s, side_r, amp_s, amp_r, scal_s, scal_r,
     edge_s, edge_r) = rest[26:36]

    own = pad.at[1, :, pl.ds(pl.multiple_of(g * R, 8), R)]
    loads = [pltpu.make_async_copy(src, dst, load_sem.at[i]) for i, (src, dst) in enumerate(
        [(obj, own), (amp.at[0], amps.at[g]), *zip((probe_in, *tables_in), loaded)])]
    for load in loads:
        load.start()
    barrier = pltpu.get_barrier_semaphore()
    count = 0
    for dt in range(T):
        for dg in range(G):
            if (dt or dg) and (dt == 0 or (dt % 2 == 0 and dg == 0)):
                pl.semaphore_signal(
                    barrier, inc=1,
                    device_id={"tile": lax.rem(t + dt, T), "group": lax.rem(g + dg, G)},
                    device_id_type=MESH)
                count += 1
    for to, there in ((t - 1, t > 0), (t + 1, t < T - 1)):
        @pl.when(there)
        def _():
            pl.semaphore_signal(barrier, inc=1, device_id={"tile": to, "group": g}, device_id_type=MESH)
    scal = scal_all
    line = lax.broadcasted_iota(jnp.int32, scal_in.shape, 0)
    scal_in[...] = jnp.where(line == 0, scalars[0][0], jnp.where(line == 1, scalars[1][0], scalars[2][0]))
    edges_here = (t > 0).astype(jnp.int32) + (t < T - 1).astype(jnp.int32)
    pl.semaphore_wait(barrier, count + edges_here)
    loads[0].wait()

    def span(group):
        return pl.ds(pl.multiple_of(group * R, 8), R)

    def to_peer(j, ch, arriving):
        peer = lax.rem(g + (G - j if arriving else j), G)
        slot = pad.at[1, ch, span(peer if arriving else g)]
        n = 2 * (j - 1) + ch
        return remote(slot, slot, own_s.at[n], own_r.at[n], t, peer)

    def to_side(j, ch, right, arriving):
        who = lax.rem(g + G - j, G)
        block = (0 if right else 2)
        dst = pad.at[block, ch, span(who)]
        src = pad.at[1, ch, span(who)]
        n = 4 * j + 2 * ch + int(right)
        return remote(dst if arriving else src, dst, side_s.at[n], side_r.at[n],
                      (t + 1 if right else t - 1) if not arriving else (t - 1 if right else t + 1), g)

    def amp_copy(j, arriving):
        peer = lax.rem(g + (G - j if arriving else j), G)
        slot = amps.at[peer if arriving else g]
        return remote(slot, slot, amp_s.at[j - 1], amp_r.at[j - 1], t, peer)

    def scal_copy(j, arriving):
        peer = lax.rem(g + (G - j if arriving else j), G)
        slot = scal.at[peer if arriving else g]
        return remote(slot if arriving else scal_in, slot, scal_s.at[j - 1], scal_r.at[j - 1], t, peer)

    def edge_copy(src, dst, right, base, arriving):
        n = base + int(right)
        side = dst.at[0 if right else 1]
        if arriving:
            return remote(side, side, edge_s.at[n], edge_r.at[n], t - 1 if right else t + 1, g)
        return remote(src.at[2 if right else 0], side, edge_s.at[n], edge_r.at[n],
                      t + 1 if right else t - 1, g)

    not_first, not_last = t > 0, t < T - 1

    for j in range(1, G):
        scal_copy(j, False).start()
    for ch in range(2):
        for j in range(1, G):
            to_peer(j, ch, False).start()
    for ch in range(2):
        pl.when(not_first)(lambda: to_side(0, ch, False, False).start())
        pl.when(not_last)(lambda: to_side(0, ch, True, False).start())
    loads[1].wait()
    for j in range(1, G):
        amp_copy(j, False).start()

    scal[g] = scal_in[...]

    @pl.when(t == 0)
    def _():
        pad[0] = jnp.zeros(pad.shape[1:], F32)
        edge[0] = jnp.zeros(edge.shape[1:], F32)
        edge_light[0] = jnp.zeros(edge_light.shape[1:], F32)

    @pl.when(t == T - 1)
    def _():
        pad[2] = jnp.zeros(pad.shape[1:], F32)
        edge[1] = jnp.zeros(edge.shape[1:], F32)
        edge_light[1] = jnp.zeros(edge_light.shape[1:], F32)

    spare = rows - W
    blocks = W // B
    terms[:, :, 0:spare] = jnp.zeros((2, blocks, spare, B), F32)
    terms[:, :, spare + W:] = jnp.zeros((2, blocks, spare, B), F32)
    light_terms[:, 0:spare] = jnp.zeros((blocks, spare, B), F32)
    light_terms[:, spare + W:] = jnp.zeros((blocks, spare, B), F32)

    def hold(ref, value):
        for b in range(blocks):
            ref[b, spare:spare + W] = value[:, b * B:(b + 1) * B]

    for load in loads[2:]:
        load.wait()
    probe_light = probe[0] * probe[0] + probe[1] * probe[1]
    hold(light_terms, probe_light)
    light_max = jnp.max(probe_light) + 1e-06

    def numbers(k):
        return scal[k, 0, 0], scal[k, 1, 0], scal[k, 2, 0].astype(F32)

    def placed(ref, row, column):
        first = g * R + spare - row
        pieces = [ref[b, pl.ds(first, R), :] for b in range(blocks)]
        wide = jnp.concatenate(pieces + [jnp.zeros((R, 3 * B - W), F32)], axis=1)
        return pltpu.roll(wide, column, 1)

    acc[...] = jnp.zeros(acc.shape, F32)
    acc_light[...] = jnp.zeros(acc_light.shape, F32)
    grad_sum[...] = jnp.zeros(grad_sum.shape, F32)
    for j in range(1, G):
        scal_copy(j, True).wait_recv()

    @pl.loop(0, G)
    def _(k):
        row, column, weight = numbers(k)
        spread = weight * placed(light_terms, row, column)
        for b in range(3):
            acc_light[b] += spread[:, b * B:(b + 1) * B]

    for ch in range(2):
        for j in range(1, G):
            to_peer(j, ch, True).wait_recv()
            pl.when(not_first)(lambda: to_side(j, ch, False, False).start())
            pl.when(not_last)(lambda: to_side(j, ch, True, False).start())
    pl.when(not_first)(lambda: edge_copy(acc_light, edge_light, False, 0, False).start())
    pl.when(not_last)(lambda: edge_copy(acc_light, edge_light, True, 0, False).start())
    for j in range(G):
        for ch in range(2):
            pl.when(not_last)(lambda: to_side(j, ch, False, True).wait_recv())
            pl.when(not_first)(lambda: to_side(j, ch, True, True).wait_recv())

    def look(j, light):
        k = lax.rem(g + j, G)
        row, column, weight = numbers(k)
        for ch in range(2):
            wide = jnp.concatenate([pad[b, ch, pl.ds(row, W), :] for b in range(3)], axis=1)
            win[k, ch] = pltpu.roll(wide, lax.rem(3 * B - column, 3 * B), 1)[:, 0:W]
        return light + weight * (win[k, 0] * win[k, 0] + win[k, 1] * win[k, 1])

    light = lax.fori_loop(0, G, look, jnp.zeros((W, W), F32))
    light_red.put(0, light)
    light_red.start_pair()

    def forth(k):
        wr, wi = win[k, 0], win[k, 1]
        pr, pi = probe[0], probe[1]
        x = jnp.concatenate([pr * wr - pi * wi, pr * wi + pi * wr], axis=0)
        y = table_left(a_head[...], a_tail[...], x)
        z = table_right(jnp.concatenate([y[:W], y[W:]], axis=1), b_head[...], b_tail[...])
        zr, zi = z[:, :W], z[:, W:]
        factor = 1.0 - amps[k] * lax.rsqrt(jnp.maximum(zr * zr + zi * zi, 0.0625))
        far[0:W], far[W:] = zr * factor, zi * factor

    def back(k, final=False):
        row, column, weight = numbers(k)
        wr, wi = win[k, 0], win[k, 1]
        pr, pi = probe[0], probe[1]
        x = far[...]
        y = table_left(b_head[...], b_tail[...], x)
        z = table_right(jnp.concatenate([y[:W], y[W:]], axis=1), a_head[...], a_tail[...])
        mr, mi = z[:, :W] * weight, z[:, W:] * weight
        sums = (grad_sum[0] + (wr * mr + wi * mi), grad_sum[1] + (wr * mi - wi * mr))
        for ch in range(2):
            if final:
                grad_red.put(ch, sums[ch])
            else:
                grad_sum[ch] = sums[ch]
        if final:
            grad_red.start_pair()
        hold(terms.at[0], pr * mr + pi * mi)
        hold(terms.at[1], pr * mi - pi * mr)
        for ch in range(2):
            spread = placed(terms.at[ch], row, column)
            for b in range(3):
                acc[b, ch] += spread[:, b * B:(b + 1) * B]

    forth(g)
    light_red.start_spread()
    back(g, G == 1)
    for j in range(1, G):
        amp_copy(j, True).wait_recv()

    def both(j):
        back(lax.rem(g + j, G))
        forth(lax.rem(g + j + 1, G))

    if G > 1:
        forth(lax.rem(g + 1, G))
        light_red.start_collect()
        pl.loop(1, G - 1)(both)
        back(lax.rem(g + G - 1, G), True)
    else:
        light_red.start_collect()

    grad_red.start_spread()
    pl.when(not_first)(lambda: edge_copy(acc, edge, False, 2, False).start())
    pl.when(not_last)(lambda: edge_copy(acc, edge, True, 2, False).start())
    light_red.relay()
    grad_red.start_collect()

    light_red.finish()
    light = light_red.get(0)
    below = 1.0 / (light + 0.25 * jnp.mean(light) + 1e-05)
    grad_red.relay()
    for src, dst, base in ((acc_light, edge_light, 0), (acc, edge, 2)):
        pl.when(not_last)(lambda: edge_copy(src, dst, False, base, True).wait_recv())
        pl.when(not_first)(lambda: edge_copy(src, dst, True, base, True).wait_recv())
    share = 1.0 / (acc_light[1] + edge_light[0] + edge_light[1] + 0.25 * light_max)
    for ch in range(2):
        new_obj[ch] = own[ch] - (acc[1, ch] + edge[0, ch] + edge[1, ch]) * share
    grad_red.finish()
    for ch in range(2):
        new_probe[ch] = probe[ch] - grad_red.get(ch) * below

    for j in range(1, G):
        for ch in range(2):
            to_peer(j, ch, False).wait_send()
        amp_copy(j, False).wait_send()
        scal_copy(j, False).wait_send()
    for j in range(G):
        for ch in range(2):
            pl.when(not_first)(lambda: to_side(j, ch, False, False).wait_send())
            pl.when(not_last)(lambda: to_side(j, ch, True, False).wait_send())
    for src, dst, base in ((acc_light, edge_light, 0), (acc, edge, 2)):
        pl.when(not_first)(lambda: edge_copy(src, dst, False, base, False).wait_send())
        pl.when(not_last)(lambda: edge_copy(src, dst, True, base, False).wait_send())


def put(obj, probe, obj_out, probe_out, sems):
    copies = [pltpu.make_async_copy(obj, obj_out, sems.at[0]),
              pltpu.make_async_copy(probe, probe_out, sems.at[1])]
    for copy in copies:
        copy.start()
    for copy in copies:
        copy.wait()


def local(T, G, object_field, probe_field, amplitudes, row_start, column_start, live_slots):
    R, B = object_field.shape[1:]
    W = probe_field.shape[1]
    rows = R * G
    H = T // 2
    gs = max(n for n in range(1, G + 1) if G % n == 0 and n * H * 8 <= W // 2)
    chunk = W // 2 // (H * gs)
    head, tail = dft_tables(W)
    spare = rows - W
    dma = lambda n: pltpu.SemaphoreType.DMA((max(n, 1),))

    def reduce_scratch(channels):
        return [
            pltpu.VMEM((2, gs, H, channels, chunk, W), F32),
            pltpu.VMEM((H, channels, chunk, W), F32),
            pltpu.VMEM((H, channels, chunk, W), F32),
            pltpu.VMEM((H - 1, channels, chunk, W), F32),
            pltpu.VMEM((2, gs, H, channels, chunk, W), F32),
            dma(1), dma(1), dma(H - 1), dma(H - 1), dma(gs * H), dma(gs * H), dma(gs * H), dma(gs * H),
        ]

    vmem_limit = 67043328 - 4 * (object_field.size + probe_field.size) - 65536
    smem = pl.BlockSpec(memory_space=pltpu.SMEM)
    hbm = pl.BlockSpec(memory_space=pltpu.HBM)
    vmem = pl.BlockSpec(memory_space=pltpu.VMEM)
    new_obj, new_probe = pl.pallas_call(
        functools.partial(kernel, T, G, gs),
        out_shape=(pltpu.VMEM(object_field.shape, F32), pltpu.VMEM(probe_field.shape, F32)),
        in_specs=[smem] * 3 + [hbm] * 7,
        out_specs=(vmem, vmem),
        scratch_shapes=[
            pltpu.VMEM((8, 128), jnp.int32),
            pltpu.VMEM(probe_field.shape, F32),
            *[pltpu.VMEM(head.shape, BF16)] * 4,
            dma(7),
            pltpu.VMEM((2 * W, W), F32),
            pltpu.VMEM((3, 2, rows, B), F32),
            pltpu.VMEM((G, W, W), F32),
            pltpu.VMEM((G, 8, 128), jnp.int32),
            pltpu.VMEM((G, 2, W, W), F32),
            pltpu.VMEM((2, W // B, W + 2 * spare, B), F32),
            pltpu.VMEM((W // B, W + 2 * spare, B), F32),
            pltpu.VMEM((3, 2, R, B), F32),
            pltpu.VMEM((3, R, B), F32),
            pltpu.VMEM((2, 2, R, B), F32),
            pltpu.VMEM((2, R, B), F32),
            pltpu.VMEM((2, W, W), F32),
            *reduce_scratch(1),
            *reduce_scratch(2),
            dma(2 * G - 2), dma(2 * G - 2), dma(4 * G), dma(4 * G), dma(G - 1), dma(G - 1),
            dma(G - 1), dma(G - 1), dma(4), dma(4),
        ],
        compiler_params=pltpu.CompilerParams(
            collective_id=0, has_side_effects=True, vmem_limit_bytes=vmem_limit),
    )(row_start, column_start, live_slots, object_field, probe_field, amplitudes, head, tail,
      head.T, tail.T)
    anywhere = pl.BlockSpec(memory_space=pl.ANY)
    return pl.pallas_call(
        put,
        out_shape=(jax.ShapeDtypeStruct(object_field.shape, F32),
                   jax.ShapeDtypeStruct(probe_field.shape, F32)),
        in_specs=[vmem] * 2,
        out_specs=(anywhere, anywhere),
        scratch_shapes=[dma(2)],
        compiler_params=pltpu.CompilerParams(vmem_limit_bytes=1024 * 1024),
    )(new_obj, new_probe)


def solution(mesh):
    return jax.shard_map(
        functools.partial(local, mesh.shape["tile"], mesh.shape["group"]),
        mesh=mesh,
        in_specs=(
            P(None, "group", "tile"),
            P(),
            P(("tile", "group"), None, None),
            P(("tile", "group")),
            P(("tile", "group")),
            P(("tile", "group")),
        ),
        out_specs=(P(None, "group", "tile"), P()),
        check_vma=False,
    )
```
